32 devices in a mesh: blk: 8 (over y, x, core), col: 4 (over z).
Axes of the slice: x: 2, y: 2, z: 4, core: 2. Of those that a mesh axis runs over, the one named last changes fastest.
Arguments:
- pixel_factors: float32 [128, 256, 128], P('blk', 'col'), may hold values from -6 to 6
- column_factors: float32 [2048, 128], P('blk'), may hold values from -0.5 to 0.5
- adagrad_state: float32 [2048, 128], P('blk'), may hold values from 0.0001 to 0.001
- observed: bfloat16 [2, 128, 256, 256], P(None, 'blk', 'col'), may hold values from -6 to 6
- mask_words: int32 [2, 128, 8192], P(None, 'blk', 'col'), may hold values from 0 to 255
- column_order: int32 [2, 256], replicated, may hold values from 0 to 255, each once within a row
Outputs:
- pixel_out: float32 [128, 256, 128], P('blk', 'col')
- column_out: float32 [2048, 128], P('blk')
The draws below stay inside these ranges and needn't reach their ends.
Inputs may be any that keep to these rules, and one draw needn't show every extreme that they name: `column_order`: each row is a permutation of 0 to 255.
All inputs are finite; a program needn't handle non-finite values.
Results may differ from the reference program's by a relative error of at most 0.0023.
Values may be sent and summed in bfloat16 or wider, within the bound.
A program may use at most 64 MiB of HBM per device.

```python
import math
import jax
import jax.numpy as jnp
from jax import lax

R = 128
CB = 256
TH = 16
STRATA = 2
INNER = 4
CW = 32
NPR = 128
NPC = 256
NCOLS = 2048
N_BLK = 8


def place_ends(drawn, own_key, least, largest):
    longest = drawn.shape.index(max(drawn.shape))
    spots = []
    for shift in (0, 1):
        where = [jax.random.randint(jax.random.fold_in(own_key, axis), (), 0, length) for axis, length in enumerate(drawn.shape)]
        where[longest] = (where[longest] + shift) % drawn.shape[longest]
        spots.append(tuple(where))
    return drawn.at[spots[0]].set(least).at[spots[1]].set(largest)


def shard_levels(key, extent, cuts, low, largest):
    def one(axis_at, shards_of):
        draws = jax.random.uniform(jax.random.fold_in(jax.random.fold_in(key, 6), axis_at), (shards_of,), jnp.float32, low / len(cuts), largest / len(cuts))
        return jnp.repeat(jnp.exp(draws), extent[axis_at] // shards_of).reshape((-1,) + (1,) * (len(extent) - axis_at - 1))

    loudness = one(*cuts[0])
    for cut in cuts[1:]:
        loudness = loudness * one(*cut)
    return loudness


def normal_values(key, shape, width, most, split=(), kind=jnp.bfloat16):
    entries = width * jax.random.normal(key, shape, jnp.float32)
    if split:
        entries = entries * shard_levels(key, shape, split, -0.22, 0.18)
    return jnp.clip(entries, -most, most).astype(kind)


def setup_inputs(seed: int = 0) -> dict:
    keys = jax.random.split(jax.random.key(seed), 7)
    pixel_factors = normal_values(keys[0], (NPR, NPC, R), 1.0, 6.0, ((0, 8), (1, 4)), jnp.float32)
    column_factors = normal_values(keys[1], (NCOLS, R), R ** -0.5, 0.5, ((0, 8),), jnp.float32)
    adagrad_state = jnp.clip(jnp.exp(math.log(0.001) - 2.3025852 * jax.random.uniform(keys[2], (NCOLS, R), jnp.float32) ** shard_levels(keys[2], (NCOLS, R), ((0, 8),), -0.2, 0.2)), 0.0001, 0.001)
    observed = normal_values(keys[3], (STRATA, NPR, NPC, CB), 1.0, 6.0, ((1, 8), (2, 4)))
    mask_words = place_ends(jax.random.randint(keys[4], (STRATA, NPR, NPC * CW), 0, 256), jax.random.fold_in(keys[4], 1), 0, 255).astype(jnp.int32)
    column_order = jax.vmap(lambda own: jax.random.permutation(own, CB))(jax.random.split(keys[5], STRATA)).reshape((STRATA, CB)).astype(jnp.int32)
    return dict(pixel_factors=pixel_factors, column_factors=column_factors, adagrad_state=adagrad_state, observed=observed, mask_words=mask_words, column_order=column_order)


def unpack_bits(words):
    shifts = jnp.arange(8, dtype=jnp.int32)
    bits = jnp.right_shift(words[:, :, None], shifts) & 1
    return bits.reshape(words.shape[0] * words.shape[1] // CW, CB)

def laplace(field):
    padded = jnp.pad(field, ((1, 1), (1, 1), (0, 0)))
    beside = padded[2:, 1:-1] + padded[:-2, 1:-1] + padded[1:-1, 2:] + padded[1:-1, :-2]
    return 4.0 * field - beside

def reference(pixel_factors, column_factors, adagrad_state, observed, mask_words, column_order):
    field = pixel_factors
    blocks = column_factors.reshape(N_BLK, CB, R)
    states = adagrad_state.reshape(N_BLK, CB, R)
    for stratum in range(STRATA):
        if stratum > 0:
            blocks = jnp.roll(blocks, 1, axis=0)
            states = jnp.roll(states, 1, axis=0)
        order = column_order[stratum]
        values = observed[stratum].reshape(N_BLK, TH, NPC, CB)
        words = mask_words[stratum].reshape(N_BLK, TH, NPC * CW)
        for step in range(INNER):
            lap = laplace(field)
            tiles = field.reshape(N_BLK, TH, NPC, R)

            def per_tile(item):
                tile, block, value, word = item
                ub = tile.reshape(TH * NPC, R).astype(jnp.bfloat16)
                placed = jnp.take(block, order, axis=0).astype(jnp.bfloat16)
                pred = jnp.dot(ub, placed.T, preferred_element_type=jnp.float32)
                marks = unpack_bits(word).astype(jnp.float32)
                resid = (marks * (pred - value.reshape(TH * NPC, CB).astype(jnp.float32))).astype(jnp.bfloat16)
                grad_tile = jnp.dot(resid, placed, preferred_element_type=jnp.float32)
                grad_cols = jnp.dot(resid.T, ub, preferred_element_type=jnp.float32) / (TH * NPC)
                return (grad_tile.reshape(TH, NPC, R), grad_cols)
            grad_tiles, grad_cols = lax.map(per_tile, (tiles, blocks, values, words))
            grad_field = grad_tiles.reshape(NPR, NPC, R) + 1.0 * lap
            grad_blocks = jnp.zeros_like(blocks).at[:, order].set(grad_cols)
            field = field - 0.1 * grad_field
            states = states + grad_blocks * grad_blocks
            blocks = blocks - 0.03 * grad_blocks / jnp.sqrt(states)
    return (field, blocks.reshape(N_BLK * CB, R))
```

```python
import functools

import jax
import jax.numpy as jnp
from jax import lax
from jax.experimental import pallas as pl
from jax.experimental.pallas import tpu as pltpu
from jax.sharding import PartitionSpec as P

INNER = 4
MESH = pl.DeviceIdType.MESH
F32 = jnp.float32
BF16 = jnp.bfloat16


def mm(a, b, dims=((1,), (0,))):
    return lax.dot_general(a, b, (dims, ((), ())), preferred_element_type=F32)


def kernel(nb, nc, u_hbm, v_hbm, g_hbm, obs_hbm, words_hbm, order_hbm,
           uout_hbm, vout_hbm,
           u, ub, ubt, obs, marks, words, order, spread, err, vin, gin, vst, gst,
           pbuf, gsend, rsbuf, psend, vfull, hrow, hcol, edge,
           in_sem, out_sem, rs_send, rs_recv, ag_send, ag_recv, h_send, h_recv,
           sh_send, sh_recv, st_send, st_recv, vf_send, vf_recv):
    _, rows, cols, rank = u.shape
    strata = obs.shape[0]
    pixels, block = err.shape
    share = rank // nc
    last = strata * INNER - 1
    scale = 1.0 / (pixels * nc)
    b = lax.axis_index("blk")
    z = lax.axis_index("col")
    up, down = lax.rem(b + nb - 1, nb), lax.rem(b + 1, nb)
    left, right = lax.rem(z + nc - 1, nc), lax.rem(z + 1, nc)
    peers = [lax.rem(z + d, nc) for d in range(nc)]

    loads = {}
    for k, (name, src, dst) in enumerate((
            ("order", order_hbm, order), ("words", words_hbm.at[0], words.at[0]),
            ("v", v_hbm, vin), ("u", u_hbm, u.at[0]), ("obs", obs_hbm.at[0], obs.at[0]),
            ("g", g_hbm, gin))):
        loads[name] = pltpu.make_async_copy(src, dst, in_sem.at[k])
    for s in range(1, strata):
        loads["words%d" % s] = pltpu.make_async_copy(words_hbm.at[s], words.at[s], in_sem.at[4 + 2 * s])
        loads["obs%d" % s] = pltpu.make_async_copy(obs_hbm.at[s], obs.at[s], in_sem.at[5 + 2 * s])
    for c in loads.values():
        c.start()

    barrier = pltpu.get_barrier_semaphore()
    greet = [(b, peers[d]) for d in range(1, nc)]
    greet += [(up, peers[d]) for d in range(nc)] + [(down, peers[d]) for d in range(nc)]
    for who in greet:
        pl.semaphore_signal(barrier, inc=1, device_id=who, device_id_type=MESH)

    def my_rows(ref, owner):
        return ref.at[pl.ds(pl.multiple_of(owner * share, share), share)]

    def remote(src, dst, ss, rs, who):
        return pltpu.make_async_remote_copy(
            src_ref=src, dst_ref=dst, send_sem=ss, recv_sem=rs, device_id=who, device_id_type=MESH)

    cw = block // 8
    per = 128 // cw
    chunks = 8 // per

    def prepare(s):
        taken = order[s:s + 1, :]
        hot = (lax.broadcasted_iota(jnp.int32, (block, block), 0) == taken).astype(F32).astype(BF16)
        lane = lax.broadcasted_iota(jnp.int32, (128, block), 0)
        col = lax.broadcasted_iota(jnp.int32, (128, block), 1)
        base = (lane % cw == col // 8).astype(F32).astype(BF16)
        sel = mm(base, hot, ((1,), (1,))).astype(BF16)
        place = (lax.broadcasted_iota(jnp.int32, (8, block), 1) % 8).astype(F32).astype(BF16)
        shift = mm(place, hot, ((1,), (1,))).astype(jnp.int32)[0:1, :]
        sub = lax.broadcasted_iota(jnp.int32, (8, 128), 0)
        lan = lax.broadcasted_iota(jnp.int32, (8, 128), 1)
        keep = (sub % per) == (lan // cw)

        def eight(h, carry):
            for r in range(8):
                for t in range(cols // 8):
                    tile = None
                    for q in range(chunks):
                        at = (t * chunks + q) * 128
                        got = words[s, pl.ds(pl.multiple_of(h * 8, 8), 8), at:at + 128][r:r + 1, :]
                        got = jnp.broadcast_to(got, (8, 128))
                        tile = got if tile is None else jnp.where(sub >= q * per, got, tile)
                    spread[r * cols + t * 8:r * cols + t * 8 + 8, :] = jnp.where(keep, tile, 0).astype(F32)
            big = mm(spread[...].astype(BF16), sel).astype(jnp.int32)
            bits = jnp.right_shift(big, jnp.broadcast_to(shift, big.shape)) & 1
            at = pl.multiple_of(h * 8 * cols, 8 * cols)
            marks[s, pl.ds(at, 8 * cols), :] = bits.astype(F32).astype(BF16)
            part = pl.ds(h * 8, 8)
            seen = obs[s, part].reshape(8 * cols, block)
            obs[s, part] = mm(seen, hot, ((1,), (1,))).astype(BF16).reshape(8, cols, block)
            return carry

        lax.fori_loop(0, rows // 8, eight, 0)

    def hold(slot):
        def pair(q, carry):
            two = u[slot, pl.ds(2 * q, 2)].reshape(2 * cols, rank)
            at = pl.multiple_of(q * 2 * cols, 2 * cols)
            ub[pl.ds(at, 2 * cols), :] = two.astype(BF16)
            ubt[:, pl.ds(at, 2 * cols)] = two.T.astype(BF16)
            return carry
        lax.fori_loop(0, rows // 2, pair, 0)
        for i in range(rows):
            edge[0, i:i + 1, :] = u[slot, i, 0:1, :]
            edge[1, i:i + 1, :] = u[slot, i, cols - 1:cols, :]

    def halos(t):
        slot = t % 2
        return [
            remote(u.at[slot, rows - 1], hrow.at[slot, 0], h_send.at[0], h_recv.at[slot, 0], (down, z)),
            remote(u.at[slot, 0], hrow.at[slot, 1], h_send.at[1], h_recv.at[slot, 1], (up, z)),
            remote(edge.at[1], hcol.at[slot, 0], h_send.at[2], h_recv.at[slot, 2], (b, right)),
            remote(edge.at[0], hcol.at[slot, 1], h_send.at[3], h_recv.at[slot, 3], (b, left)),
        ]

    loads["order"].wait()
    loads["words"].wait()
    loads["obs"].wait()
    prepare(0)
    loads["u"].wait()
    hold(0)
    loads["v"].wait()
    vfull[...] = vin[...].T
    pbuf[0] = vfull[...].astype(BF16)
    vst[0] = vfull[pl.ds(pl.multiple_of(z * share, share), share), :]
    loads["g"].wait()
    vfull[...] = gin[...].T
    gst[0] = vfull[pl.ds(pl.multiple_of(z * share, share), share), :]

    pl.semaphore_wait(barrier, len(greet))
    moving = halos(0)
    for c in moving:
        c.start()

    has = [(b > 0).astype(F32), (b < nb - 1).astype(F32), (z > 0).astype(F32), (z < nc - 1).astype(F32)]
    rs = ag = None
    big = min(256, pixels)

    for t in range(last + 1):
        s, slot = t // INNER, t % 2
        pt = pbuf.at[s * 2 + slot]
        nxt = pbuf.at[((t + 1) // INNER) * 2 + (t + 1) % 2] if t < last else None
        total = None
        for k in range(pixels // big):
            at = k * big
            pred = mm(ub[at:at + big, :], pt[...])
            seen = obs[s, at // cols:(at + big) // cols].reshape(big, block).astype(F32)
            e = (marks[s, at:at + big, :].astype(F32) * (pred - seen)).astype(BF16)
            err[at:at + big, :] = e
            part = mm(ubt[:, at:at + big], e)
            total = part if total is None else total + part
        vfull[...] = total
        gsend[...] = total.astype(BF16)
        rs = [remote(my_rows(gsend, peers[d]), rsbuf.at[s, d - 1], rs_send.at[d - 1], rs_recv.at[s, d - 1],
                     (b, peers[d])) for d in range(1, nc)]
        for c in rs:
            c.start()

        for c in moving:
            c.wait()

        new = 1 - slot
        first_col = lax.broadcasted_iota(jnp.int32, (cols, rank), 0) == 0
        last_col = lax.broadcasted_iota(jnp.int32, (cols, rank), 0) == cols - 1
        for i in range(rows):
            me = u[slot, i]
            above = u[slot, i - 1] if i > 0 else hrow[slot, 0] * has[0]
            below = u[slot, i + 1] if i < rows - 1 else hrow[slot, 1] * has[1]
            before = jnp.where(first_col, hcol[slot, 0, i:i + 1, :] * has[2], pltpu.roll(me, 1, 0))
            after = jnp.where(last_col, hcol[slot, 1, i:i + 1, :] * has[3], pltpu.roll(me, cols - 1, 0))
            lap = 4.0 * me - (above + below + before + after)
            grad = mm(err[i * cols:(i + 1) * cols, :], pt[...], ((1,), (1,))) + lap
            u[new, i] = me - 0.1 * grad
        if t < last:
            hold(new)
            moving = halos(t + 1)
            for c in moving:
                c.start()
        else:
            out_u = pltpu.make_async_copy(u.at[new], uout_hbm, out_sem.at[0])
            out_u.start()

        for c in rs:
            c.wait()
        g = vfull[pl.ds(pl.multiple_of(z * share, share), share), :]
        for d in range(1, nc):
            g = g + rsbuf[s, d - 1].astype(F32)
        g = g * scale
        if t > 0 and t % INNER == 0:
            for c in carry_state:
                c.wait()
        state = gst[s] + g * g
        fac = vst[s] - 0.03 * g / jnp.sqrt(state)
        if ag is not None:
            for c in ag:
                c.wait_send()
        if t == last:
            mine = my_rows(vfull, z)
            mine[...] = fac
            ag = [remote(mine, mine, vf_send.at[d - 1], vf_recv.at[d - 1], (b, peers[d]))
                  for d in range(1, nc)]
            for c in ag:
                c.start()
            for c in ag:
                c.wait()
        elif (t + 1) % INNER:
            gst[s] = state
            vst[s] = fac
            psend[...] = fac.astype(BF16)
            ag = [remote(psend, my_rows(nxt, z), ag_send.at[d - 1], ag_recv.at[d - 1], (b, peers[d]))
                  for d in range(1, nc)]
            for c in ag:
                c.start()
            my_rows(nxt, z)[...] = fac.astype(BF16)
            for c in ag:
                c.wait_recv()
        else:
            gst[s] = state
            vst[s] = fac
            psend[...] = fac.astype(BF16)
            ag = [remote(psend, my_rows(nxt, z), sh_send.at[s, d], sh_recv.at[s, d], (down, peers[d]))
                  for d in range(nc)]
            carry_state = [
                remote(vst.at[s], vst.at[s + 1], st_send.at[s, 0], st_recv.at[s, 0], (down, z)),
                remote(gst.at[s], gst.at[s + 1], st_send.at[s, 1], st_recv.at[s, 1], (down, z)),
            ]
            for c in ag + carry_state:
                c.start()
            loads["words%d" % (s + 1)].wait()
            loads["obs%d" % (s + 1)].wait()
            prepare(s + 1)
            for c in ag:
                c.wait_recv()

    vin[...] = vfull[...].T
    out_v = pltpu.make_async_copy(vin, vout_hbm, out_sem.at[1])
    out_v.start()
    out_u.wait()
    out_v.wait()


def local(nb, nc, pixel_factors, column_factors, adagrad_state, observed, mask_words, column_order):
    rows, cols, rank = pixel_factors.shape
    block = column_factors.shape[0]
    strata = observed.shape[0]
    pixels = rows * cols
    share = rank // nc
    dma = pltpu.SemaphoreType.DMA
    return pl.pallas_call(
        functools.partial(kernel, nb, nc),
        out_shape=(
            jax.ShapeDtypeStruct((rows, cols, rank), F32),
            jax.ShapeDtypeStruct((block, rank), F32),
        ),
        in_specs=[pl.BlockSpec(memory_space=pl.ANY)] * 6,
        out_specs=(pl.BlockSpec(memory_space=pl.ANY),) * 2,
        scratch_shapes=[
            pltpu.VMEM((2, rows, cols, rank), F32),
            pltpu.VMEM((pixels, rank), BF16),
            pltpu.VMEM((rank, pixels), BF16),
            pltpu.VMEM((strata, rows, cols, block), BF16),
            pltpu.VMEM((strata, pixels, block), BF16),
            pltpu.VMEM((strata,) + mask_words.shape[1:], jnp.int32),
            pltpu.VMEM((strata, block), jnp.int32),
            pltpu.VMEM((8 * cols, 128), F32),
            pltpu.VMEM((pixels, block), BF16),
            pltpu.VMEM((block, rank), F32),
            pltpu.VMEM((block, rank), F32),
            pltpu.VMEM((strata, share, block), F32),
            pltpu.VMEM((strata, share, block), F32),
            pltpu.VMEM((2 * strata, rank, block), BF16),
            pltpu.VMEM((rank, block), BF16),
            pltpu.VMEM((strata, nc - 1, share, block), BF16),
            pltpu.VMEM((share, block), BF16),
            pltpu.VMEM((rank, block), F32),
            pltpu.VMEM((2, 2, cols, rank), F32),
            pltpu.VMEM((2, 2, rows, rank), F32),
            pltpu.VMEM((2, rows, rank), F32),
            dma((4 + 2 * strata,)), dma((2,)),
            dma((nc - 1,)), dma((strata, nc - 1)), dma((nc - 1,)), dma((nc - 1,)),
            dma((4,)), dma((2, 4)),
            dma((strata, nc)), dma((strata, nc)), dma((strata, 2)), dma((strata, 2)),
            dma((nc - 1,)), dma((nc - 1,)),
        ],
        compiler_params=pltpu.CompilerParams(
            collective_id=0, has_side_effects=True, vmem_limit_bytes=32 * 1024 * 1024
        ),
        name="sgd",
    )(pixel_factors, column_factors, adagrad_state, observed, mask_words, column_order)


def solution(mesh):
    placed = (
        P("blk", "col", None),
        P("blk", None),
        P("blk", None),
        P(None, "blk", "col", None),
        P(None, "blk", "col"),
        P(),
    )
    return jax.shard_map(
        functools.partial(local, mesh.shape["blk"], mesh.shape["col"]),
        mesh=mesh,
        in_specs=placed,
        out_specs=(P("blk", "col", None), P("blk", None)),
        check_vma=False,
    )
```

```python
import functools

import jax
import jax.numpy as jnp
from jax import lax
from jax.experimental import pallas as pl
from jax.experimental.pallas import tpu as pltpu
from jax.sharding import PartitionSpec as P

INNER = 4
PARTS = 2
MESH = pl.DeviceIdType.MESH
F32 = jnp.float32
BF16 = jnp.bfloat16


def mm(a, b, dims=((1,), (0,))):
    return lax.dot_general(a, b, (dims, ((), ())), preferred_element_type=F32)


def kernel(nb, nc, u_hbm, v_hbm, g_hbm, obs_hbm, words_hbm, order_hbm,
           uout_hbm, vout_hbm,
           u, ub, ubt, obs, marks, words, order, spread, err, vin, gin, vst, gst,
           pbuf, rsbuf, hrow, hcol, edge,
           in_sem, out_sem, rs_send, rs_recv, h_send, h_recv, st_send, st_recv):
    _, rows, cols, rank = u.shape
    strata = obs.shape[0]
    pixels, block = err.shape
    half = block // PARTS
    last = strata * INNER - 1
    scale = 1.0 / (pixels * nc)
    b = lax.axis_index("blk")
    z = lax.axis_index("col")
    up, down = lax.rem(b + nb - 1, nb), lax.rem(b + 1, nb)
    left, right = lax.rem(z + nc - 1, nc), lax.rem(z + 1, nc)
    high = (2 * z) // nc
    others = []
    for k in range(nc - 1):
        fall = nc - 1 - k
        fall = fall - (z >= fall).astype(jnp.int32)
        rise = k + (z <= k).astype(jnp.int32)
        others.append(fall + high * (rise - fall))

    loads = {}
    for k, (name, src, dst) in enumerate((
            ("order", order_hbm, order), ("words", words_hbm.at[0], words.at[0]),
            ("v", v_hbm, vin), ("u", u_hbm, u.at[0]), ("obs", obs_hbm.at[0], obs.at[0]),
            ("g", g_hbm, gin))):
        loads[name] = pltpu.make_async_copy(src, dst, in_sem.at[k])
    for s in range(1, strata):
        loads["words%d" % s] = pltpu.make_async_copy(words_hbm.at[s], words.at[s], in_sem.at[4 + 2 * s])
        loads["obs%d" % s] = pltpu.make_async_copy(obs_hbm.at[s], obs.at[s], in_sem.at[5 + 2 * s])
    for c in loads.values():
        c.start()

    barrier = pltpu.get_barrier_semaphore()
    greet = [(b, who) for who in others] + [(up, z), (down, z)]
    for who in greet:
        pl.semaphore_signal(barrier, inc=1, device_id=who, device_id_type=MESH)

    def remote(src, dst, ss, rs, who):
        return pltpu.make_async_remote_copy(
            src_ref=src, dst_ref=dst, send_sem=ss, recv_sem=rs, device_id=who, device_id_type=MESH)

    cw = block // 8
    per = 128 // cw
    chunks = 8 // per

    def prepare(s):
        taken = order[s:s + 1, :]
        hot = (lax.broadcasted_iota(jnp.int32, (block, block), 0) == taken).astype(F32).astype(BF16)
        lane = lax.broadcasted_iota(jnp.int32, (128, block), 0)
        col = lax.broadcasted_iota(jnp.int32, (128, block), 1)
        base = (lane % cw == col // 8).astype(F32).astype(BF16)
        sel = mm(base, hot, ((1,), (1,))).astype(BF16)
        place = (lax.broadcasted_iota(jnp.int32, (8, block), 1) % 8).astype(F32).astype(BF16)
        shift = mm(place, hot, ((1,), (1,))).astype(jnp.int32)[0:1, :]
        sub = lax.broadcasted_iota(jnp.int32, (8, 128), 0)
        lan = lax.broadcasted_iota(jnp.int32, (8, 128), 1)
        keep = (sub % per) == (lan // cw)

        def eight(h, carry):
            for r in range(8):
                for t in range(cols // 8):
                    tile = None
                    for q in range(chunks):
                        at = (t * chunks + q) * 128
                        got = words[s, pl.ds(pl.multiple_of(h * 8, 8), 8), at:at + 128][r:r + 1, :]
                        got = jnp.broadcast_to(got, (8, 128))
                        tile = got if tile is None else jnp.where(sub >= q * per, got, tile)
                    spread[r * cols + t * 8:r * cols + t * 8 + 8, :] = jnp.where(keep, tile, 0).astype(F32)
            big = mm(spread[...].astype(BF16), sel).astype(jnp.int32)
            bits = jnp.right_shift(big, jnp.broadcast_to(shift, big.shape)) & 1
            at = pl.multiple_of(h * 8 * cols, 8 * cols)
            marks[s, pl.ds(at, 8 * cols), :] = bits.astype(F32).astype(BF16)
            part = pl.ds(h * 8, 8)
            seen = obs[s, part].reshape(8 * cols, block)
            obs[s, part] = mm(seen, hot, ((1,), (1,))).astype(BF16).reshape(8, cols, block)
            return carry

        lax.fori_loop(0, rows // 8, eight, 0)

    def hold(slot):
        def pair(q, carry):
            two = u[slot, pl.ds(2 * q, 2)].reshape(2 * cols, rank)
            at = pl.multiple_of(q * 2 * cols, 2 * cols)
            ub[pl.ds(at, 2 * cols), :] = two.astype(BF16)
            ubt[:, pl.ds(at, 2 * cols)] = two.T.astype(BF16)
            return carry
        lax.fori_loop(0, rows // 2, pair, 0)
        for i in range(rows):
            edge[0, i:i + 1, :] = u[slot, i, 0:1, :]
            edge[1, i:i + 1, :] = u[slot, i, cols - 1:cols, :]

    def halos(t):
        slot = t % 2
        return [
            remote(u.at[slot, rows - 1], hrow.at[slot, 0], h_send.at[0], h_recv.at[slot, 0], (down, z)),
            remote(u.at[slot, 0], hrow.at[slot, 1], h_send.at[1], h_recv.at[slot, 1], (up, z)),
            remote(edge.at[1], hcol.at[slot, 0], h_send.at[2], h_recv.at[slot, 2], (b, right)),
            remote(edge.at[0], hcol.at[slot, 1], h_send.at[3], h_recv.at[slot, 3], (b, left)),
        ]

    loads["order"].wait()
    loads["words"].wait()
    loads["obs"].wait()
    prepare(0)
    loads["u"].wait()
    hold(0)
    loads["v"].wait()
    vst[0] = vin[...].T
    pbuf[0] = vst[0].astype(BF16)
    loads["g"].wait()
    gst[0] = gin[...].T

    pl.semaphore_wait(barrier, len(greet))
    moving = halos(0)
    for c in moving:
        c.start()

    has = [(b > 0).astype(F32), (b < nb - 1).astype(F32), (z > 0).astype(F32), (z < nc - 1).astype(F32)]
    big = min(256, pixels)
    sums = [None] * PARTS
    passed = []
    out_v = []

    def lanes(h):
        return slice(h * half, (h + 1) * half)

    def finish(t, h):
        s, at = t // INNER, lanes(h)
        for c in sums[h]:
            c.wait()
        if t > 0 and t % INNER == 0:
            for c in passed[s - 1][h]:
                c.wait()
        g = rsbuf[h, t % 2, 0].astype(F32)
        for k in range(1, nc):
            g = g + rsbuf[h, t % 2, k].astype(F32)
        g = g * scale
        state = gst[s, :, at] + g * g
        fac = vst[s, :, at] - 0.03 * g / jnp.sqrt(state)
        if t == last:
            vin[at, :] = fac.T
            c = pltpu.make_async_copy(vin.at[pl.ds(h * half, half)], vout_hbm.at[pl.ds(h * half, half)], out_sem.at[1 + h])
            c.start()
            out_v.append(c)
            return
        pbuf[s, :, at] = fac.astype(BF16)
        gst[s, :, at] = state
        vst[s, :, at] = fac
        if (t + 1) % INNER == 0:
            lot = []
            for k, ref in enumerate((pbuf, vst, gst)):
                lot.append(remote(ref.at[s, :, pl.ds(h * half, half)], ref.at[s + 1, :, pl.ds(h * half, half)],
                                  st_send.at[s, h, k], st_recv.at[s, h, k], (down, z)))
                lot[-1].start()
            lot[0].wait()
            passed[s].append(lot[1:])

    for t in range(last + 1):
        s, slot = t // INNER, t % 2
        passed.append([])
        for h in range(PARTS):
            if t > 0:
                finish(t - 1, h)
            total = None
            for k in range(pixels // big):
                at = k * big
                pred = mm(ub[at:at + big, :], pbuf[s, :, lanes(h)])
                seen = obs[s, at // cols:(at + big) // cols, :, lanes(h)].reshape(big, half).astype(F32)
                e = (marks[s, at:at + big, lanes(h)].astype(F32) * (pred - seen)).astype(BF16)
                err[at:at + big, lanes(h)] = e
                part = mm(ubt[:, at:at + big], e)
                total = part if total is None else total + part
            mine = rsbuf.at[h, slot, z]
            mine[...] = total.astype(BF16)
            sums[h] = []
            for k, who in enumerate(others):
                c = remote(mine, mine, rs_send.at[h, k], rs_recv.at[h, slot, z], (b, who))
                c.start()
                came = remote(mine, rsbuf.at[h, slot, who], rs_send.at[h, k], rs_recv.at[h, slot, who], (b, who))
                sums[h].append(came)

        for c in moving:
            c.wait()
        new = 1 - slot
        first_col = lax.broadcasted_iota(jnp.int32, (cols, rank), 0) == 0
        last_col = lax.broadcasted_iota(jnp.int32, (cols, rank), 0) == cols - 1
        for i in range(rows):
            me = u[slot, i]
            above = u[slot, i - 1] if i > 0 else hrow[slot, 0] * has[0]
            below = u[slot, i + 1] if i < rows - 1 else hrow[slot, 1] * has[1]
            before = jnp.where(first_col, hcol[slot, 0, i:i + 1, :] * has[2], pltpu.roll(me, 1, 0))
            after = jnp.where(last_col, hcol[slot, 1, i:i + 1, :] * has[3], pltpu.roll(me, cols - 1, 0))
            lap = 4.0 * me - (above + below + before + after)
            grad = mm(err[i * cols:(i + 1) * cols, :], pbuf[s], ((1,), (1,))) + lap
            u[new, i] = me - 0.1 * grad
        if t < last:
            hold(new)
            moving = halos(t + 1)
            for c in moving:
                c.start()
        else:
            out_u = pltpu.make_async_copy(u.at[new], uout_hbm, out_sem.at[0])
            out_u.start()
        if t % INNER == 1 and s + 1 < strata:
            loads["words%d" % (s + 1)].wait()
            loads["obs%d" % (s + 1)].wait()
            prepare(s + 1)

    for h in range(PARTS):
        finish(last, h)
    out_u.wait()
    for c in out_v:
        c.wait()


def local(nb, nc, pixel_factors, column_factors, adagrad_state, observed, mask_words, column_order):
    rows, cols, rank = pixel_factors.shape
    block = column_factors.shape[0]
    strata = observed.shape[0]
    pixels = rows * cols
    dma = pltpu.SemaphoreType.DMA
    return pl.pallas_call(
        functools.partial(kernel, nb, nc),
        out_shape=(
            jax.ShapeDtypeStruct((rows, cols, rank), F32),
            jax.ShapeDtypeStruct((block, rank), F32),
        ),
        in_specs=[pl.BlockSpec(memory_space=pl.ANY)] * 6,
        out_specs=(pl.BlockSpec(memory_space=pl.ANY),) * 2,
        scratch_shapes=[
            pltpu.VMEM((2, rows, cols, rank), F32),
            pltpu.VMEM((pixels, rank), BF16),
            pltpu.VMEM((rank, pixels), BF16),
            pltpu.VMEM((strata, rows, cols, block), BF16),
            pltpu.VMEM((strata, pixels, block), BF16),
            pltpu.VMEM((strata,) + mask_words.shape[1:], jnp.int32),
            pltpu.VMEM((strata, block), jnp.int32),
            pltpu.VMEM((8 * cols, 128), F32),
            pltpu.VMEM((pixels, block), BF16),
            pltpu.VMEM((block, rank), F32),
            pltpu.VMEM((block, rank), F32),
            pltpu.VMEM((strata, rank, block), F32),
            pltpu.VMEM((strata, rank, block), F32),
            pltpu.VMEM((strata, rank, block), BF16),
            pltpu.VMEM((PARTS, 2, nc, rank, block // PARTS), BF16),
            pltpu.VMEM((2, 2, cols, rank), F32),
            pltpu.VMEM((2, 2, rows, rank), F32),
            pltpu.VMEM((2, rows, rank), F32),
            dma((4 + 2 * strata,)), dma((1 + PARTS,)),
            dma((PARTS, nc - 1)), dma((PARTS, 2, nc)),
            dma((4,)), dma((2, 4)),
            dma((strata, PARTS, 3)), dma((strata, PARTS, 3)),
        ],
        compiler_params=pltpu.CompilerParams(
            collective_id=0, has_side_effects=True, vmem_limit_bytes=60 * 1024 * 1024
        ),
        name="sgd",
    )(pixel_factors, column_factors, adagrad_state, observed, mask_words, column_order)


def solution(mesh):
    placed = (
        P("blk", "col", None),
        P("blk", None),
        P("blk", None),
        P(None, "blk", "col", None),
        P(None, "blk", "col"),
        P(),
    )
    return jax.shard_map(
        functools.partial(local, mesh.shape["blk"], mesh.shape["col"]),
        mesh=mesh,
        in_specs=placed,
        out_specs=(P("blk", "col", None), P("blk", None)),
        check_vma=False,
    )
```

```python
import functools

import jax
import jax.numpy as jnp
from jax import lax
from jax.experimental import pallas as pl
from jax.experimental.pallas import tpu as pltpu
from jax.sharding import PartitionSpec as P

INNER = 4
PARTS = 2
MESH = pl.DeviceIdType.MESH
F32 = jnp.float32
BF16 = jnp.bfloat16


def mm(a, b, dims=((1,), (0,))):
    return lax.dot_general(a, b, (dims, ((), ())), preferred_element_type=F32)


def kernel(nb, nc, u_hbm, v_hbm, g_hbm, obs_hbm, words_hbm, order_hbm,
           uout_hbm, vout_hbm,
           u, ub, ubt, obs, marks, words, order, spread, err, vin, gin, vst, gst,
           pbuf, rsbuf, hrow, hcol, edge,
           in_sem, out_sem, rs_send, rs_recv, h_send, h_recv, st_send, st_recv):
    _, rows, cols, rank = u.shape
    strata = obs.shape[0]
    pixels, block = err.shape
    half = block // PARTS
    last = strata * INNER - 1
    scale = 1.0 / (pixels * nc)
    b = lax.axis_index("blk")
    z = lax.axis_index("col")
    up, down = lax.rem(b + nb - 1, nb), lax.rem(b + 1, nb)
    left, right = lax.rem(z + nc - 1, nc), lax.rem(z + 1, nc)
    high = (2 * z) // nc
    others = []
    for k in range(nc - 1):
        fall = nc - 1 - k
        fall = fall - (z >= fall).astype(jnp.int32)
        rise = k + (z <= k).astype(jnp.int32)
        others.append(rise + high * (fall - rise))

    loads = {}
    for k, (name, src, dst) in enumerate((
            ("order", order_hbm, order), ("words", words_hbm.at[0], words.at[0]),
            ("v", v_hbm, vin), ("u", u_hbm, u.at[0]), ("obs", obs_hbm.at[0], obs.at[0]),
            ("g", g_hbm, gin))):
        loads[name] = pltpu.make_async_copy(src, dst, in_sem.at[k])
    for s in range(1, strata):
        loads["words%d" % s] = pltpu.make_async_copy(words_hbm.at[s], words.at[s], in_sem.at[4 + 2 * s])
        loads["obs%d" % s] = pltpu.make_async_copy(obs_hbm.at[s], obs.at[s], in_sem.at[5 + 2 * s])
    for c in loads.values():
        c.start()

    barrier = pltpu.get_barrier_semaphore()
    greet = [(b, who) for who in others] + [(up, z), (down, z)]
    for who in greet:
        pl.semaphore_signal(barrier, inc=1, device_id=who, device_id_type=MESH)

    def remote(src, dst, ss, rs, who):
        return pltpu.make_async_remote_copy(
            src_ref=src, dst_ref=dst, send_sem=ss, recv_sem=rs, device_id=who, device_id_type=MESH)

    cw = block // 8
    per = 128 // cw
    chunks = 8 // per

    def prepare(s):
        taken = order[s:s + 1, :]
        hot = (lax.broadcasted_iota(jnp.int32, (block, block), 0) == taken).astype(F32).astype(BF16)
        lane = lax.broadcasted_iota(jnp.int32, (128, block), 0)
        col = lax.broadcasted_iota(jnp.int32, (128, block), 1)
        base = (lane % cw == col // 8).astype(F32).astype(BF16)
        sel = mm(base, hot, ((1,), (1,))).astype(BF16)
        place = (lax.broadcasted_iota(jnp.int32, (8, block), 1) % 8).astype(F32).astype(BF16)
        shift = mm(place, hot, ((1,), (1,))).astype(jnp.int32)[0:1, :]
        sub = lax.broadcasted_iota(jnp.int32, (8, 128), 0)
        lan = lax.broadcasted_iota(jnp.int32, (8, 128), 1)
        keep = (sub % per) == (lan // cw)

        def eight(h, carry):
            for r in range(8):
                for t in range(cols // 8):
                    tile = None
                    for q in range(chunks):
                        at = (t * chunks + q) * 128
                        got = words[s, pl.ds(pl.multiple_of(h * 8, 8), 8), at:at + 128][r:r + 1, :]
                        got = jnp.broadcast_to(got, (8, 128))
                        tile = got if tile is None else jnp.where(sub >= q * per, got, tile)
                    spread[r * cols + t * 8:r * cols + t * 8 + 8, :] = jnp.where(keep, tile, 0).astype(F32)
            big = mm(spread[...].astype(BF16), sel).astype(jnp.int32)
            bits = jnp.right_shift(big, jnp.broadcast_to(shift, big.shape)) & 1
            at = pl.multiple_of(h * 8 * cols, 8 * cols)
            marks[s, pl.ds(at, 8 * cols), :] = bits.astype(F32).astype(BF16)
            part = pl.ds(h * 8, 8)
            seen = obs[s, part].reshape(8 * cols, block)
            obs[s, part] = mm(seen, hot, ((1,), (1,))).astype(BF16).reshape(8, cols, block)
            return carry

        lax.fori_loop(0, rows // 8, eight, 0)

    def hold(slot):
        def pair(q, carry):
            two = u[slot, pl.ds(2 * q, 2)].reshape(2 * cols, rank)
            at = pl.multiple_of(q * 2 * cols, 2 * cols)
            ub[pl.ds(at, 2 * cols), :] = two.astype(BF16)
            ubt[:, pl.ds(at, 2 * cols)] = two.T.astype(BF16)
            return carry
        lax.fori_loop(0, rows // 2, pair, 0)
    def halos(t):
        slot = t % 2
        return [
            remote(u.at[slot, rows - 1], hrow.at[slot, 0], h_send.at[0], h_recv.at[slot, 0], (down, z)),
            remote(u.at[slot, 0], hrow.at[slot, 1], h_send.at[1], h_recv.at[slot, 1], (up, z)),
            remote(edge.at[1], hcol.at[slot, 0], h_send.at[2], h_recv.at[slot, 2], (b, right)),
            remote(edge.at[0], hcol.at[slot, 1], h_send.at[3], h_recv.at[slot, 3], (b, left)),
        ]

    loads["order"].wait()
    loads["words"].wait()
    loads["obs"].wait()
    prepare(0)
    loads["u"].wait()
    hold(0)
    for i in range(rows):
        edge[0, i:i + 1, :] = u[0, i, 0:1, :]
        edge[1, i:i + 1, :] = u[0, i, cols - 1:cols, :]
    loads["v"].wait()
    vst[0] = vin[...].T
    pbuf[0] = vst[0].astype(BF16)
    loads["g"].wait()
    gst[0] = gin[...].T

    pl.semaphore_wait(barrier, len(greet))
    moving = halos(0)
    for c in moving:
        c.start()

    has = [(b > 0).astype(F32), (b < nb - 1).astype(F32), (z > 0).astype(F32), (z < nc - 1).astype(F32)]
    big = min(256, pixels)
    sums = [None] * PARTS
    passed = []
    out_v = []

    def lanes(h):
        return slice(h * half, (h + 1) * half)

    def finish(t, h):
        s, at = t // INNER, lanes(h)
        for c in sums[h]:
            c.wait()
        if t > 0 and t % INNER == 0:
            for c in passed[s - 1][h]:
                c.wait()
        g = rsbuf[h, t % 2, 0].astype(F32)
        for k in range(1, nc):
            g = g + rsbuf[h, t % 2, k].astype(F32)
        g = g * scale
        state = gst[s, :, at] + g * g
        fac = vst[s, :, at] - 0.03 * g / jnp.sqrt(state)
        if t == last:
            vin[at, :] = fac.T
            c = pltpu.make_async_copy(vin.at[pl.ds(h * half, half)], vout_hbm.at[pl.ds(h * half, half)], out_sem.at[1 + h])
            c.start()
            out_v.append(c)
            return
        pbuf[s, :, at] = fac.astype(BF16)
        gst[s, :, at] = state
        vst[s, :, at] = fac
        if (t + 1) % INNER == 0:
            lot = []
            for k, ref in enumerate((pbuf, vst, gst)):
                lot.append(remote(ref.at[s, :, pl.ds(h * half, half)], ref.at[s + 1, :, pl.ds(h * half, half)],
                                  st_send.at[s, h, k], st_recv.at[s, h, k], (down, z)))
                lot[-1].start()
            lot[0].wait()
            passed[s].append(lot[1:])

    for t in range(last + 1):
        s, slot = t // INNER, t % 2
        passed.append([])
        for h in range(PARTS):
            if t > 0:
                finish(t - 1, h)
            total = None
            for k in range(pixels // big):
                at = k * big
                pred = mm(ub[at:at + big, :], pbuf[s, :, lanes(h)])
                seen = obs[s, at // cols:(at + big) // cols, :, lanes(h)].reshape(big, half).astype(F32)
                e = (marks[s, at:at + big, lanes(h)].astype(F32) * (pred - seen)).astype(BF16)
                err[at:at + big, lanes(h)] = e
                part = mm(ubt[:, at:at + big], e)
                total = part if total is None else total + part
            mine = rsbuf.at[h, slot, z]
            mine[...] = total.astype(BF16)
            sums[h] = []
            for k, who in enumerate(others):
                c = remote(mine, mine, rs_send.at[h, k], rs_recv.at[h, slot, z], (b, who))
                c.start()
                came = remote(mine, rsbuf.at[h, slot, who], rs_send.at[h, k], rs_recv.at[h, slot, who], (b, who))
                sums[h].append(came)

        new = 1 - slot
        first_col = lax.broadcasted_iota(jnp.int32, (cols, rank), 0) == 0
        last_col = lax.broadcasted_iota(jnp.int32, (cols, rank), 0) == cols - 1
        for i in range(rows):
            me = u[slot, i]
            beside = jnp.where(first_col, 0.0, pltpu.roll(me, 1, 0))
            beside = beside + jnp.where(last_col, 0.0, pltpu.roll(me, cols - 1, 0))
            if i > 0:
                beside = beside + u[slot, i - 1]
            if i < rows - 1:
                beside = beside + u[slot, i + 1]
            grad = mm(err[i * cols:(i + 1) * cols, :], pbuf[s], ((1,), (1,))) + (4.0 * me - beside)
            u[new, i] = me - 0.1 * grad
        for c in moving:
            c.wait()
        u[new, 0] = u[new, 0] + hrow[slot, 0] * (0.1 * has[0])
        u[new, rows - 1] = u[new, rows - 1] + hrow[slot, 1] * (0.1 * has[1])
        for i in range(rows):
            low = u[new, i, 0:1, :] + hcol[slot, 0, i:i + 1, :] * (0.1 * has[2])
            top = u[new, i, cols - 1:cols, :] + hcol[slot, 1, i:i + 1, :] * (0.1 * has[3])
            u[new, i, 0:1, :] = low
            u[new, i, cols - 1:cols, :] = top
            edge[0, i:i + 1, :] = low
            edge[1, i:i + 1, :] = top
        if t < last:
            moving = halos(t + 1)
            for c in moving:
                c.start()
            hold(new)
        else:
            out_u = pltpu.make_async_copy(u.at[new], uout_hbm, out_sem.at[0])
            out_u.start()
        if t % INNER == 1 and s + 1 < strata:
            loads["words%d" % (s + 1)].wait()
            loads["obs%d" % (s + 1)].wait()
            prepare(s + 1)

    for h in range(PARTS):
        finish(last, h)
    out_u.wait()
    for c in out_v:
        c.wait()


def local(nb, nc, pixel_factors, column_factors, adagrad_state, observed, mask_words, column_order):
    rows, cols, rank = pixel_factors.shape
    block = column_factors.shape[0]
    strata = observed.shape[0]
    pixels = rows * cols
    dma = pltpu.SemaphoreType.DMA
    return pl.pallas_call(
        functools.partial(kernel, nb, nc),
        out_shape=(
            jax.ShapeDtypeStruct((rows, cols, rank), F32),
            jax.ShapeDtypeStruct((block, rank), F32),
        ),
        in_specs=[pl.BlockSpec(memory_space=pl.ANY)] * 6,
        out_specs=(pl.BlockSpec(memory_space=pl.ANY),) * 2,
        scratch_shapes=[
            pltpu.VMEM((2, rows, cols, rank), F32),
            pltpu.VMEM((pixels, rank), BF16),
            pltpu.VMEM((rank, pixels), BF16),
            pltpu.VMEM((strata, rows, cols, block), BF16),
            pltpu.VMEM((strata, pixels, block), BF16),
            pltpu.VMEM((strata,) + mask_words.shape[1:], jnp.int32),
            pltpu.VMEM((strata, block), jnp.int32),
            pltpu.VMEM((8 * cols, 128), F32),
            pltpu.VMEM((pixels, block), BF16),
            pltpu.VMEM((block, rank), F32),
            pltpu.VMEM((block, rank), F32),
            pltpu.VMEM((strata, rank, block), F32),
            pltpu.VMEM((strata, rank, block), F32),
            pltpu.VMEM((strata, rank, block), BF16),
            pltpu.VMEM((PARTS, 2, nc, rank, block // PARTS), BF16),
            pltpu.VMEM((2, 2, cols, rank), F32),
            pltpu.VMEM((2, 2, rows, rank), F32),
            pltpu.VMEM((2, rows, rank), F32),
            dma((4 + 2 * strata,)), dma((1 + PARTS,)),
            dma((PARTS, nc - 1)), dma((PARTS, 2, nc)),
            dma((4,)), dma((2, 4)),
            dma((strata, PARTS, 3)), dma((strata, PARTS, 3)),
        ],
        compiler_params=pltpu.CompilerParams(
            collective_id=0, has_side_effects=True, vmem_limit_bytes=60 * 1024 * 1024
        ),
        name="sgd",
    )(pixel_factors, column_factors, adagrad_state, observed, mask_words, column_order)


def solution(mesh):
    placed = (
        P("blk", "col", None),
        P("blk", None),
        P("blk", None),
        P(None, "blk", "col", None),
        P(None, "blk", "col"),
        P(),
    )
    return jax.shard_map(
        functools.partial(local, mesh.shape["blk"], mesh.shape["col"]),
        mesh=mesh,
        in_specs=placed,
        out_specs=(P("blk", "col", None), P("blk", None)),
        check_vma=False,
    )
```
